32 devices in a mesh: dp: 4 (over y, core), tensor: 8 (over z, x).
Axes of the slice: x: 2, y: 2, z: 4, core: 2. Of those that a mesh axis runs over, the one named last changes fastest.
Arguments:
- tokens: bfloat16 [512, 8192], P('dp', 'tensor'), may hold values from -6 to 6
- grad_out: bfloat16 [512, 8192], P('dp', 'tensor'), may hold values from -6 to 6
- packed_weight_blocks: float32 [2048, 128, 128], P(('dp', 'tensor')), may hold values from -4 to 4
- packed_first_moments: float32 [2048, 128, 128], P(('dp', 'tensor')), may hold values from -2 to 2
- packed_second_moments: float32 [2048, 128, 128], P(('dp', 'tensor')), may hold values from 0.05 to 1
- block_mask: int32 [2, 64, 128], P(None, None, 'tensor'), may hold values from 0 to 1, as said below
- last_step: int32 [2, 64, 128], P(None, None, 'tensor'), may hold values from 130 to 139
- regrown: int32 [2, 64, 128], P(None, None, 'tensor'), may hold values 0 or 1
- step_now: int32 [1], replicated, may hold values from 140 to 149
Outputs:
- input_grad: bfloat16 [512, 8192], P('dp', 'tensor')
- new_weights: float32 [2048, 128, 128], P(('dp', 'tensor'))
- new_first: float32 [2048, 128, 128], P(('dp', 'tensor'))
- new_second: float32 [2048, 128, 128], P(('dp', 'tensor'))
The draws below stay inside these ranges and needn't reach their ends.
Inputs may be any that keep to these rules, and one draw needn't show every extreme that they name: `block_mask`: within one tensor shard's 16 block columns, both matrices together hold between 128 and 256 active blocks; some shard holds exactly 256.
All inputs are finite; a program needn't handle non-finite values. No bound on the sum of `regrown` on one device may be relied on, other than what follows from the above.
Results may differ from the reference program's by a relative error of at most 0.014.
Values may be sent and summed in bfloat16 or wider, within the bound.
A program may use at most 192 MiB of HBM per device.

```python
import math
import jax
import jax.numpy as jnp
from jax import lax

D = 8192
BLOCK_SIDE = 128
TOK_DEV = 128
TOKENS = 512
DB = 64
HB = 128
HBT = 16
SLOTS = 256
DEVICE_SLOTS = 64
PACKED_SLOTS = 2048
N_DP = 4
N_TENSOR = 8


def draw_block_mask(key, part):
    count_key = jax.random.fold_in(key, 11)
    fullest_key = jax.random.fold_in(key, 12)
    order_key = jax.random.fold_in(key, 13)
    shard_blocks = 2 * DB * HBT
    counts = jax.random.randint(count_key, (N_TENSOR,), SLOTS // 2, SLOTS + 1, dtype=jnp.int32)
    fullest = jax.random.randint(fullest_key, (), 0, N_TENSOR, dtype=jnp.int32)
    counts = jnp.where(jnp.arange(N_TENSOR, dtype=jnp.int32) == fullest, SLOTS, counts)
    scores = jax.random.randint(order_key, (N_TENSOR, shard_blocks), 0, 1 << 18, dtype=jnp.int32)
    scores = scores * shard_blocks + jnp.arange(shard_blocks, dtype=jnp.int32)[None, :]
    block_ranks = jnp.argsort(jnp.argsort(scores, axis=1), axis=1)
    active = (block_ranks < counts[:, None]).astype(jnp.int32)
    layout = active.reshape(N_TENSOR, 2, DB, HBT)
    return layout.transpose(1, 2, 0, 3).reshape(2, DB, HB)


def set_ends(entries, rng, least, high):
    shape = entries.shape
    index_at = [jax.random.randint(jax.random.fold_in(rng, axis), (), 0, shape[axis]) for axis in range(len(shape))]
    entries = entries.at[tuple(index_at)].set(least)
    longest = shape.index(max(shape))
    index_at[longest] = (index_at[longest] + 1) % shape[longest]
    return entries.at[tuple(index_at)].set(high)


def level_of(rng, shape, shards, low, high):
    level = 1.0
    for dim, blocks in shards:
        steps = jax.random.uniform(jax.random.fold_in(jax.random.fold_in(rng, 6), dim), (blocks,), jnp.float32, low / len(shards), high / len(shards))
        level = level * jnp.repeat(jnp.exp(steps), shape[dim] // blocks).reshape((-1,) + (1,) * (len(shape) - 1 - dim))
    return level


def centred(rng, dims, deviation, bound, shards=(), kind=jnp.bfloat16):
    entries = deviation * jax.random.normal(rng, dims, jnp.float32)
    if shards:
        entries = entries * level_of(rng, dims, shards, -0.22, 0.18)
    return jnp.clip(entries, -bound, bound).astype(kind)


def setup_inputs(seed: int = 0) -> dict:
    arg_keys = jax.random.split(jax.random.key(seed), 10)
    return {
        "tokens": centred(arg_keys[0], (TOKENS, D), 1.0, 6.0, ((0, 4), (1, 8))),
        "grad_out": centred(arg_keys[1], (TOKENS, D), 1.0, 6.0, ((0, 4), (1, 8))),
        "packed_weight_blocks": centred(arg_keys[2], (PACKED_SLOTS, BLOCK_SIDE, BLOCK_SIDE), 1.0, 4.0, ((0, 32),), jnp.float32),
        "packed_first_moments": centred(arg_keys[3], (PACKED_SLOTS, BLOCK_SIDE, BLOCK_SIDE), 0.3, 2.0, ((0, 32),), jnp.float32),
        "packed_second_moments": jnp.clip(jnp.exp(math.log(1.0) - 2.9957323 * jax.random.uniform(arg_keys[4], (PACKED_SLOTS, BLOCK_SIDE, BLOCK_SIDE), jnp.float32) ** level_of(arg_keys[4], (PACKED_SLOTS, BLOCK_SIDE, BLOCK_SIDE), ((0, 32),), -0.2, 0.2)), 0.05, 1.0),
        "block_mask": draw_block_mask(jax.random.fold_in(arg_keys[9], 71), 0),
        "last_step": set_ends(jax.random.randint(arg_keys[6], (2, DB, HB), 130, 140), jax.random.fold_in(arg_keys[6], 1), 130, 139).astype(jnp.int32),
        "regrown": set_ends((jax.random.randint(arg_keys[7], (2, DB, HB), 0, 5) < 1).astype(jnp.int32), jax.random.fold_in(arg_keys[7], 1), 0, 1),
        "step_now": jax.random.randint(arg_keys[8], (1,), 140, 150).astype(jnp.int32),
    }


beta_one = 0.9
beta_two = 0.95
learn_rate = 0.05
decay_rate = 0.1
epsilon = 0.05

def silu_slope(values):
    sigmoid = jax.nn.sigmoid(values)
    return sigmoid * (1.0 + values * (1.0 - sigmoid))

def slot_table(mask_grid, regrown_grid, last_grid, slot_total):
    flags = mask_grid.reshape(-1)
    numbered = jnp.cumsum(flags, dtype=jnp.int32) - 1
    block_total = flags.shape[0]
    matches = (numbered[None, :] == jnp.arange(slot_total, dtype=jnp.int32)[:, None]) & (flags[None, :] == 1)
    block_index = lax.optimization_barrier(jnp.sum(jnp.where(matches, jnp.arange(block_total, dtype=jnp.int32)[None, :], 0), axis=1, dtype=jnp.int32))
    slot_regrown = lax.optimization_barrier(jnp.sum(jnp.where(matches, regrown_grid.reshape(-1)[None, :], 0), axis=1, dtype=jnp.int32))
    slot_last = lax.optimization_barrier(jnp.sum(jnp.where(matches, last_grid.reshape(-1)[None, :], 0), axis=1, dtype=jnp.int32))
    live_count = jnp.sum(flags, dtype=jnp.int32)
    return (numbered, block_index, slot_regrown, slot_last, live_count)

def adam_step(weights, first_in, second_in, block_grads, live_slots, slot_regrown, slot_last, step_value):
    regrown_now = (slot_regrown == 1)[:, None, None]
    skipped = (step_value - slot_last - 1).astype(jnp.float32)[:, None, None]
    base_weight = jnp.where(regrown_now, jnp.float32(0.0), weights)
    kept_first = jnp.where(regrown_now, jnp.float32(0.0), first_in * jnp.power(jnp.float32(beta_one), skipped))
    kept_second = jnp.where(regrown_now, jnp.float32(0.0), second_in * jnp.power(jnp.float32(beta_two), skipped))
    new_first = beta_one * kept_first + (1.0 - beta_one) * block_grads
    new_second = beta_two * kept_second + (1.0 - beta_two) * block_grads * block_grads
    bias_count = jnp.where(regrown_now, jnp.float32(1.0), step_value.astype(jnp.float32) + jnp.zeros_like(skipped))
    first_hat = new_first / (1.0 - jnp.power(jnp.float32(beta_one), bias_count))
    second_hat = new_second / (1.0 - jnp.power(jnp.float32(beta_two), bias_count))
    new_weight = base_weight - learn_rate * (first_hat / (jnp.sqrt(second_hat) + epsilon) + decay_rate * base_weight)
    keep_slot = live_slots[:, None, None]
    return (jnp.where(keep_slot, new_weight, weights), jnp.where(keep_slot, new_first, first_in), jnp.where(keep_slot, new_second, second_in))

def reference(tokens, grad_out, packed_weight_blocks, packed_first_moments, packed_second_moments, block_mask, last_step, regrown, step_now):
    scale_factor = 3.0 / math.sqrt(D)
    step_value = step_now[0]

    def by_shard(packed_array):
        return packed_array.reshape(N_DP, N_TENSOR, DEVICE_SLOTS, BLOCK_SIDE, BLOCK_SIDE).transpose(1, 0, 2, 3, 4).reshape(N_TENSOR, SLOTS, BLOCK_SIDE, BLOCK_SIDE)

    def grid_shard(layout):
        return layout.reshape(2, DB, N_TENSOR, HBT).transpose(2, 0, 1, 3)

    def unshard(stacked_blocks):
        return stacked_blocks.reshape(N_TENSOR, N_DP, DEVICE_SLOTS, BLOCK_SIDE, BLOCK_SIDE).transpose(1, 0, 2, 3, 4).reshape(PACKED_SLOTS, BLOCK_SIDE, BLOCK_SIDE)

    def shard_step(accum, shard_in):
        weights_s, first_s, second_s, mask_s, last_s, regrown_s = shard_in
        numbered, block_index, slot_regrown, slot_last, live_count = slot_table(mask_s, regrown_s, last_s, SLOTS)
        usable = (mask_s.reshape(-1) == 1) & (regrown_s.reshape(-1) == 0)
        packed = weights_s.astype(jnp.bfloat16)
        dense = jnp.take(packed, jnp.maximum(numbered, 0), axis=0)
        dense = jnp.where(usable[:, None, None], dense, jnp.zeros((), jnp.bfloat16))
        dense = dense.reshape(2, DB, HBT, BLOCK_SIDE, BLOCK_SIDE).transpose(0, 1, 3, 2, 4).reshape(2, D, HBT * BLOCK_SIDE)
        pre_act = scale_factor * jnp.dot(tokens, dense[0], preferred_element_type=jnp.float32)
        back_act = scale_factor * jnp.dot(grad_out, dense[1], preferred_element_type=jnp.float32)
        hidden = jax.nn.silu(pre_act).astype(jnp.bfloat16)
        hidden_grad = (back_act * silu_slope(pre_act)).astype(jnp.bfloat16)
        partial_value = (scale_factor * jnp.dot(hidden_grad, dense[0].T, preferred_element_type=jnp.float32)).astype(jnp.bfloat16)
        accum = accum + partial_value.astype(jnp.float32)
        left_source = jnp.concatenate([tokens.reshape(TOKENS, DB, BLOCK_SIDE), grad_out.reshape(TOKENS, DB, BLOCK_SIDE)], axis=1)
        right_source = jnp.concatenate([hidden_grad.reshape(TOKENS, HBT, BLOCK_SIDE), hidden.reshape(TOKENS, HBT, BLOCK_SIDE)], axis=1)
        matrix_of = block_index // (DB * HBT)
        row_of = block_index // HBT % DB
        column_of = block_index % HBT
        left_rows = jnp.take(left_source, (matrix_of * DB + row_of).astype(jnp.int32), axis=1)
        right_rows = jnp.take(right_source, (matrix_of * HBT + column_of).astype(jnp.int32), axis=1)
        left_groups = left_rows.astype(jnp.float32).reshape(N_DP, TOK_DEV, SLOTS, BLOCK_SIDE)
        right_groups = right_rows.astype(jnp.float32).reshape(N_DP, TOK_DEV, SLOTS, BLOCK_SIDE)
        group_tiles = (scale_factor * jnp.einsum('gtsi,gtsj->gsij', left_groups, right_groups)).astype(jnp.bfloat16)
        block_grads = lax.optimization_barrier(jnp.sum(group_tiles.astype(jnp.float32), axis=0))
        live_slots = jnp.arange(SLOTS, dtype=jnp.int32) < live_count
        updated = adam_step(weights_s, first_s, second_s, block_grads, live_slots, slot_regrown, slot_last, step_value)
        return (accum, updated)
    shard_inputs = (by_shard(packed_weight_blocks), by_shard(packed_first_moments), by_shard(packed_second_moments), grid_shard(block_mask), grid_shard(last_step), grid_shard(regrown))
    accum, updated = lax.scan(shard_step, jnp.zeros((TOKENS, D), jnp.float32), shard_inputs)
    new_weights, new_first, new_second = updated
    return (accum.astype(jnp.bfloat16), unshard(new_weights), unshard(new_first), unshard(new_second))
```

```python
import functools
import math

import jax
import jax.numpy as jnp
from jax import lax
from jax.experimental import pallas as pl
from jax.experimental.pallas import tpu as pltpu
from jax.sharding import PartitionSpec as P

D = 8192


beta_one = 0.9
beta_two = 0.95
learn_rate = 0.05
decay_rate = 0.1
epsilon = 0.05


def silu_slope(values):
    sigmoid = jax.nn.sigmoid(values)
    return sigmoid * (1.0 + values * (1.0 - sigmoid))


def slot_table(mask_grid, regrown_grid, last_grid, slot_total):
    codes = lax.optimization_barrier((mask_grid + 2 * regrown_grid + 4 * last_grid).reshape(-1))
    flags = codes & 1
    numbered = jnp.cumsum(flags, dtype=jnp.int32) - 1
    block_total = flags.shape[0]
    wanted = jnp.where(flags == 1, numbered, -1)
    entries = jnp.arange(block_total, dtype=jnp.int32) + block_total * (codes >> 1)
    matches = wanted[None, :] == jnp.arange(slot_total, dtype=jnp.int32)[:, None]
    found = lax.optimization_barrier(
        jnp.sum(jnp.where(matches, entries[None, :], 0), axis=1, dtype=jnp.int32)
    )
    block_index = found % block_total
    slot_regrown = found // block_total & 1
    slot_last = found // block_total // 2
    live_count = jnp.sum(flags, dtype=jnp.int32)
    up_count = jnp.sum(flags[: block_total // 2], dtype=jnp.int32)
    return (block_index, slot_regrown, slot_last, live_count, up_count)


def adam_step(
    weights, first_in, second_in, block_grads, live_slots, slot_regrown, slot_last, step_value
):
    regrown_now = (slot_regrown == 1)[:, None, None]
    skipped = (step_value - slot_last - 1).astype(jnp.float32)[:, None, None]
    base_weight = jnp.where(regrown_now, jnp.float32(0.0), weights)
    kept_first = jnp.where(
        regrown_now, jnp.float32(0.0), first_in * jnp.power(jnp.float32(beta_one), skipped)
    )
    kept_second = jnp.where(
        regrown_now, jnp.float32(0.0), second_in * jnp.power(jnp.float32(beta_two), skipped)
    )
    new_first = beta_one * kept_first + (1.0 - beta_one) * block_grads
    new_second = beta_two * kept_second + (1.0 - beta_two) * block_grads * block_grads
    bias_count = jnp.where(
        regrown_now, jnp.float32(1.0), step_value.astype(jnp.float32) + jnp.zeros_like(skipped)
    )
    first_hat = new_first / (1.0 - jnp.power(jnp.float32(beta_one), bias_count))
    second_hat = new_second / (1.0 - jnp.power(jnp.float32(beta_two), bias_count))
    new_weight = base_weight - learn_rate * (
        first_hat / (jnp.sqrt(second_hat) + epsilon) + decay_rate * base_weight
    )
    keep_slot = live_slots[:, None, None]
    return (
        jnp.where(keep_slot, new_weight, weights),
        jnp.where(keep_slot, new_first, first_in),
        jnp.where(keep_slot, new_second, second_in),
    )


INNER = 2
UNROLL = 8


def piece(index, chunk, chunks, shard):
    size = shard // chunks
    return pl.ds((index * chunks + chunk) * size, size)


def remote(src, dst, send_sem, recv_sem, axis, target):
    return pltpu.make_async_remote_copy(
        src_ref=src,
        dst_ref=dst,
        send_sem=send_sem,
        recv_sem=recv_sem,
        device_id={axis: target},
        device_id_type=pl.DeviceIdType.MESH,
    )


def greet(targets, meanwhile):
    barrier = pltpu.get_barrier_semaphore()
    for axis, target in targets:
        pl.semaphore_signal(
            barrier, inc=1, device_id={axis: target}, device_id_type=pl.DeviceIdType.MESH
        )
    meanwhile()
    pl.semaphore_wait(barrier, len(targets))


class LineGather:
    def __init__(self, axis, size, chunks, shard, out, sems):
        self.axis, self.chunks, self.out = axis, chunks, out
        self.recv, self.up, self.down, self.across = sems
        self.outer = size // INNER
        me = lax.axis_index(axis)
        self.me, self.mine, self.inner = me, me // INNER, me % INNER
        self.shard = shard

    def copy(self, source, chunk, way, inner=None):
        inner = self.inner if inner is None else inner
        index = source * INNER + inner
        at = self.out.at[piece(index, chunk, self.chunks, self.shard)]
        slot = source * self.chunks + chunk
        sem, target = {
            "up": (self.up, self.me + INNER),
            "down": (self.down, self.me - INNER),
            "across": (self.across, self.mine * INNER + 1 - self.inner),
        }[way]
        recv = self.recv.at[index * self.chunks + chunk]
        return remote(at, at, sem.at[slot], recv, self.axis, target)

    def wait_recv(self, source, chunk, inner):
        self.copy(source, chunk, "across", inner).wait_recv()

    def begin(self, chunk):
        mine = self.mine

        @pl.when(mine + 1 < self.outer)
        def _():
            self.copy(mine, chunk, "up").start()

        @pl.when(mine > 0)
        def _():
            self.copy(mine, chunk, "down").start()

        self.copy(mine, chunk, "across").start()

    def step(self, distance, chunk):
        low, high = self.mine - distance, self.mine + distance

        @pl.when(low >= 0)
        def _():
            self.wait_recv(low, chunk, self.inner)

            @pl.when(self.mine + 1 < self.outer)
            def _():
                self.copy(low, chunk, "up").start()

            self.copy(low, chunk, "across").start()

        @pl.when(high < self.outer)
        def _():
            self.wait_recv(high, chunk, self.inner)

            @pl.when(self.mine > 0)
            def _():
                self.copy(high, chunk, "down").start()

            self.copy(high, chunk, "across").start()

    def arrive(self, source):
        for chunk in range(self.chunks):
            self.wait_recv(source, chunk, 1 - self.inner)

    def finish(self):
        for source in range(self.outer):
            for chunk in range(self.chunks):
                self.copy(source, chunk, "across").wait_send()

                @pl.when((self.mine >= source) & (self.mine + 1 < self.outer))
                def _(source=source, chunk=chunk):
                    self.copy(source, chunk, "up").wait_send()

                @pl.when((self.mine <= source) & (self.mine > 0))
                def _(source=source, chunk=chunk):
                    self.copy(source, chunk, "down").wait_send()


class PairReduce:
    def __init__(self, axis, size, chunks, data, out, near, far, sems):
        self.axis, self.chunks, self.data, self.out = axis, chunks, data, out
        self.near, self.far = near, far
        self.near_send, self.near_recv, self.far_send, self.far_recv = sems
        self.outer = size // INNER
        me = lax.axis_index(axis)
        self.me, self.mine, self.inner = me, me // INNER, me % INNER
        self.shard = out.shape[0]
        self.size = self.shard // chunks

    def owner(self, offset):
        return lax.rem(self.mine + offset, self.outer)

    def targets(self):
        far = [
            (self.axis, self.owner(offset) * INNER + self.inner)
            for offset in range(1, self.outer)
        ]
        return far + [(self.axis, self.mine * INNER + 1 - self.inner)]

    def first(self, offset, chunk, inner):
        return ((self.owner(offset) * INNER + inner) * self.chunks + chunk) * self.size

    def near_copy(self, offset, chunk):
        owner = self.owner(offset)
        other = 1 - self.inner
        slot = owner * self.chunks + chunk
        return remote(
            self.data.at[piece(owner * INNER + other, chunk, self.chunks, self.shard)],
            self.near.at[piece(owner, chunk, self.chunks, self.shard)],
            self.near_send.at[slot],
            self.near_recv.at[slot],
            self.axis,
            self.mine * INNER + other,
        )

    def far_copy(self, offset, chunk):
        owner = self.owner(offset)
        return remote(
            self.near.at[piece(owner, chunk, self.chunks, self.shard)],
            self.far.at[piece(offset - 1, chunk, self.chunks, self.shard)],
            self.far_send.at[(offset - 1) * self.chunks + chunk],
            self.far_recv.at[(offset - 1) * self.chunks + chunk],
            self.axis,
            owner * INNER + self.inner,
        )

    def send_pair(self, offset, chunk):
        self.near_copy(offset, chunk).wait_recv()
        near_at = (self.owner(offset) * self.chunks + chunk) * self.size
        data_at = self.first(offset, chunk, self.inner)

        def add(index, carry):
            total = self.near[near_at + index].astype(jnp.float32)
            total += self.data[data_at + index].astype(jnp.float32)
            self.near[near_at + index] = total.astype(jnp.bfloat16)
            return carry

        lax.fori_loop(0, self.size, add, 0)
        self.far_copy(offset, chunk).start()

    def total(self, chunk):
        self.near_copy(0, chunk).wait_recv()
        for offset in range(1, self.outer):
            self.far_copy(offset, chunk).wait_recv()
        size = self.size
        near_at = (self.mine * self.chunks + chunk) * size
        data_at = (self.me * self.chunks + chunk) * size

        def add(index, carry):
            total = self.near[near_at + index].astype(jnp.float32)
            total += self.data[data_at + index].astype(jnp.float32)
            for offset in range(1, self.outer):
                at = ((offset - 1) * self.chunks + chunk) * size
                total += self.far[at + index].astype(jnp.float32)
            self.out[chunk * size + index] = total.astype(self.out.dtype)
            return carry

        lax.fori_loop(0, size, add, 0)

    def finish(self):
        for chunk in range(self.chunks):
            for offset in range(self.outer):
                self.near_copy(offset, chunk).wait_send()
                if offset > 0:
                    self.far_copy(offset, chunk).wait_send()


def chain_products(count, product, chain, table, previous):
    unroll = math.gcd(UNROLL, count)

    def step(index, carry):
        base = index * unroll
        parts = [product(base + k) for k in range(unroll)]
        for k in range(unroll):
            chain[base + k + 1] = parts[k] + chain[table[previous + base + k]]
        return carry

    lax.fori_loop(0, count // unroll, step, 0)


def make_tiles(table, right_table, left_ref, right_ref, tiles_ref, first, count, scale):
    unroll = math.gcd(UNROLL, count)

    def step(index, carry):
        base = first + index * unroll
        for k in range(unroll):
            tile = lax.dot_general(
                left_ref[table[base + k]],
                right_ref[table[right_table + base + k]],
                (((0,), (0,)), ((), ())),
                preferred_element_type=jnp.float32,
            )
            tiles_ref[base + k] = (scale * tile).astype(jnp.bfloat16)
        return carry

    lax.fori_loop(0, count // unroll, step, 0)


def step_kernel(
    sizes,
    gather_chunks,
    reduce_chunks,
    scale,
    table,
    weights,
    tokens,
    grad_out,
    grads_out,
    rows_out,
    packed,
    left,
    stage,
    chain,
    right,
    tiles,
    rows,
    wide_near,
    wide_far,
    thin_near,
    thin_far,
    *sems,
):
    local, sems = sems[:2], sems[2:]
    owned, side = stage.shape[0], stage.shape[1]
    slot_total, columns, row_blocks = packed.shape[0], right.shape[0] // 2, rows.shape[0]
    local_rows = rows_out.shape[0]
    line = LineGather("dp", sizes[0], gather_chunks[0], owned, packed, sems[:4])
    wing = LineGather("tensor", sizes[1], gather_chunks[1], 2 * local_rows, left, sems[4:8])
    wide = PairReduce(
        "dp", sizes[0], reduce_chunks[0], tiles, grads_out, wide_near, wide_far, sems[8:12]
    )
    thin = PairReduce(
        "tensor", sizes[1], reduce_chunks[1], rows, rows_out, thin_near, thin_far, sems[12:]
    )
    right_table = slot_total
    column_table = 2 * slot_total
    row_table = 3 * slot_total
    column_last = 4 * slot_total
    row_last = column_last + 2 * columns

    def load_left(index):
        source = tokens if index < local_rows else grad_out
        return pltpu.make_async_copy(
            source.at[:, pl.ds(index % local_rows * side, side)],
            left.at[wing.me * 2 * local_rows + index],
            local[0].at[index],
        )

    def load_weights(chunk):
        at = piece(0, chunk, line.chunks, owned)
        return pltpu.make_async_copy(weights.at[at], stage.at[at], local[1].at[chunk])

    def round_weights(chunk):
        load_weights(chunk).wait()
        size = owned // line.chunks
        at = chunk * size
        mine = line.me * owned + at

        def round_block(index, carry):
            packed[mine + index] = stage[at + index].astype(jnp.bfloat16)
            return carry

        lax.fori_loop(0, size, round_block, 0)

    for index in range(2 * local_rows):
        load_left(index).start()
    for chunk in range(line.chunks):
        load_weights(chunk).start()

    def meanwhile():
        chain[0] = jnp.zeros(chain.shape[1:], jnp.float32)
        for index in range(2 * local_rows):
            load_left(index).wait()
        for chunk in range(line.chunks):
            round_weights(chunk)

    greet(wide.targets() + thin.targets(), meanwhile)

    events = []
    for gather, weight in ((line, 1.5), (wing, 1.0)):
        for chunk in range(gather.chunks):
            gather.begin(chunk)
            for distance in range(1, gather.outer):
                passed = (distance - 1 + (chunk + 1) / gather.chunks) / (gather.outer - 1)
                events.append((weight * passed, gather, distance, chunk))
    events.sort(key=lambda event: event[0])
    for _, gather, distance, chunk in events:
        gather.step(distance, chunk)
    for source in range(wing.outer):
        wing.arrive(source)
    for source in range(line.outer):
        line.arrive(source)

    def forward(slot):
        return jnp.dot(
            left[table[slot]], packed[slot], preferred_element_type=jnp.float32
        )

    chain_products(slot_total, forward, chain, table, column_table)

    def activate(column, carry):
        pre_act = scale * chain[table[column_last + column]]
        back_act = scale * chain[table[column_last + columns + column]]
        right[column] = (back_act * silu_slope(pre_act)).astype(jnp.bfloat16)
        right[columns + column] = jax.nn.silu(pre_act).astype(jnp.bfloat16)
        return carry

    lax.fori_loop(0, columns, activate, 0)

    def backward(slot):
        return lax.dot_general(
            right[table[right_table + slot]],
            packed[slot],
            (((1,), (1,)), ((), ())),
            preferred_element_type=jnp.float32,
        )

    def sum_rows():
        chain_products(slot_total, backward, chain, table, row_table)

        def finish(index, carry):
            rows[index] = (scale * chain[table[row_last + index]]).astype(jnp.bfloat16)
            return carry

        lax.fori_loop(0, row_blocks, finish, 0)
        for offset in list(range(1, thin.outer)) + [0]:
            for chunk in range(thin.chunks):
                thin.near_copy(offset, chunk).start()

    def tiles_of(offset, chunk, inner):
        first = wide.first(offset, chunk, inner)
        make_tiles(table, right_table, left, right, tiles, first, wide.size, scale)

    far_steps = [(o, k) for o in range(1, wide.outer) for k in range(wide.chunks)]
    last_far = len(far_steps) - 1
    for at, step in enumerate(far_steps):
        tiles_of(*step, 1 - wide.inner)
        wide.near_copy(*step).start()
        if at > 0:
            wide.send_pair(*far_steps[at - 1])
        tiles_of(*step, wide.inner)
        if at == min(2, last_far):
            sum_rows()
    wide.send_pair(*far_steps[-1])
    thin_pairs = [(o, k) for o in range(1, thin.outer) for k in range(thin.chunks)]
    for chunk in range(wide.chunks):
        tiles_of(0, chunk, 1 - wide.inner)
        wide.near_copy(0, chunk).start()
        tiles_of(0, chunk, wide.inner)
        low = chunk * len(thin_pairs) // wide.chunks
        high = (chunk + 1) * len(thin_pairs) // wide.chunks
        for pair in thin_pairs[low:high]:
            thin.send_pair(*pair)
    for chunk in range(wide.chunks - 1):
        wide.total(chunk)
    for chunk in range(thin.chunks):
        thin.total(chunk)
    wide.total(wide.chunks - 1)
    line.finish()
    wing.finish()
    wide.finish()
    thin.finish()


def run_step(table, weights, tokens, grad_out, columns, row_blocks, scale):
    sizes = (lax.axis_size("dp"), lax.axis_size("tensor"))
    owned, side = weights.shape[0], weights.shape[1]
    tok_count = tokens.shape[0]
    local_rows = tokens.shape[1] // side
    slot_total = owned * sizes[0]
    outer = [size // INNER for size in sizes]
    gather_chunks = (math.gcd(8, owned), math.gcd(4, 2 * local_rows))
    reduce_chunks = (math.gcd(8, owned), math.gcd(2, local_rows))
    block = (tok_count, side)
    tile = (side, side)
    dma = pltpu.SemaphoreType.DMA

    def scratch(count, shape, kind=jnp.bfloat16):
        return pltpu.VMEM((count,) + shape, kind)

    shapes = [
        scratch(slot_total, tile),
        scratch(2 * local_rows * sizes[1], block),
        scratch(owned, tile, jnp.float32),
        scratch(slot_total + 1, block, jnp.float32),
        scratch(2 * columns, block),
        scratch(slot_total, tile),
        scratch(row_blocks, block),
        scratch(outer[0] * owned, tile),
        scratch(max(outer[0] - 1, 1) * owned, tile),
        scratch(outer[1] * local_rows, block),
        scratch(max(outer[1] - 1, 1) * local_rows, block),
        dma((2 * local_rows,)),
        dma((gather_chunks[0],)),
    ]
    for size, chunks in zip(sizes, gather_chunks):
        shapes += [dma((size * chunks,))] + [dma((size // INNER * chunks,))] * 3
    for count, chunks in zip(outer, reduce_chunks):
        shapes += [dma((count * chunks,))] * 2 + [dma((max(count - 1, 1) * chunks,))] * 2
    vmem = pl.BlockSpec(memory_space=pltpu.VMEM)
    smem = pl.BlockSpec(memory_space=pltpu.SMEM)
    anywhere = pl.BlockSpec(memory_space=pl.ANY)
    return pl.pallas_call(
        functools.partial(step_kernel, sizes, gather_chunks, reduce_chunks, scale),
        out_shape=(
            jax.ShapeDtypeStruct((owned,) + tile, jnp.float32),
            jax.ShapeDtypeStruct((local_rows,) + block, jnp.bfloat16),
        ),
        in_specs=[smem, anywhere, anywhere, anywhere],
        out_specs=(vmem, vmem),
        scratch_shapes=shapes,
        compiler_params=pltpu.CompilerParams(
            collective_id=0, has_side_effects=True, vmem_limit_bytes=62 * 1024 * 1024
        ),
    )(table, weights, tokens, grad_out)


def last_where(matches):
    places = jnp.arange(1, matches.shape[1] + 1, dtype=jnp.int32)
    return jnp.max(jnp.where(matches, places[None, :], 0), axis=1)


def per_device(
    tokens,
    grad_out,
    packed_weight_blocks,
    packed_first_moments,
    packed_second_moments,
    block_mask,
    last_step,
    regrown,
    step_now,
):
    scale_factor = 3.0 / math.sqrt(D)
    tok_count = tokens.shape[0]
    owned_slots = packed_weight_blocks.shape[0]
    block_size = packed_weight_blocks.shape[1]
    row_blocks = block_mask.shape[1]
    column_blocks = block_mask.shape[2]
    local_rows = tokens.shape[1] // block_size
    groups = lax.axis_size("dp")
    slot_total = owned_slots * groups
    step_value = step_now[0]
    block_index, slot_regrown, slot_last, live_count, _ = slot_table(
        block_mask, regrown, last_step, slot_total
    )
    matrix_of = block_index // (row_blocks * column_blocks)
    row_of = block_index // column_blocks % row_blocks
    column_of = block_index % column_blocks
    slot_ids = jnp.arange(slot_total, dtype=jnp.int32)
    usable = (slot_ids < live_count) & (slot_regrown == 0)
    left_at = (row_of // local_rows * 2 + matrix_of) * local_rows + row_of % local_rows
    right_at = matrix_of * column_blocks + column_of
    column_key = jnp.where(usable, right_at, -1)
    row_key = jnp.where(usable & (matrix_of == 0), row_of, -1)
    earlier = slot_ids[None, :] < slot_ids[:, None]
    table = jnp.concatenate(
        [
            left_at,
            right_at,
            last_where((right_at[:, None] == column_key[None, :]) & earlier),
            last_where((row_of[:, None] == row_key[None, :]) & earlier),
            last_where(jnp.arange(2 * column_blocks, dtype=jnp.int32)[:, None] == column_key),
            last_where(jnp.arange(row_blocks, dtype=jnp.int32)[:, None] == row_key),
        ]
    )
    block_grads, summed_rows = run_step(
        table,
        packed_weight_blocks,
        tokens,
        grad_out,
        column_blocks,
        row_blocks,
        scale_factor,
    )
    input_grad = (
        summed_rows.transpose(1, 0, 2).reshape(tok_count, tokens.shape[1]).astype(jnp.bfloat16)
    )
    owner_first = lax.axis_index("dp") * owned_slots
    mine_regrown = lax.dynamic_slice_in_dim(slot_regrown, owner_first, owned_slots)
    mine_last = lax.dynamic_slice_in_dim(slot_last, owner_first, owned_slots)
    live_slots = owner_first + jnp.arange(owned_slots, dtype=jnp.int32) < live_count
    new_weights, new_first, new_second = adam_step(
        packed_weight_blocks,
        packed_first_moments,
        packed_second_moments,
        block_grads,
        live_slots,
        mine_regrown,
        mine_last,
        step_value,
    )
    return (input_grad, new_weights, new_first, new_second)


def solution(mesh):
    in_specs = (
        P("dp", "tensor"),
        P("dp", "tensor"),
        P(("dp", "tensor"), None, None),
        P(("dp", "tensor"), None, None),
        P(("dp", "tensor"), None, None),
        P(None, None, "tensor"),
        P(None, None, "tensor"),
        P(None, None, "tensor"),
        P(),
    )
    out_specs = (
        P("dp", "tensor"),
        P(("dp", "tensor"), None, None),
        P(("dp", "tensor"), None, None),
        P(("dp", "tensor"), None, None),
    )
    return jax.shard_map(
        per_device, mesh=mesh, in_specs=in_specs, out_specs=out_specs, check_vma=False
    )
```

```python
import functools
import math

import jax
import jax.numpy as jnp
from jax import lax
from jax.experimental import pallas as pl
from jax.experimental.pallas import tpu as pltpu
from jax.sharding import PartitionSpec as P

D = 8192


beta_one = 0.9
beta_two = 0.95
learn_rate = 0.05
decay_rate = 0.1
epsilon = 0.05


def silu_slope(values):
    sigmoid = jax.nn.sigmoid(values)
    return sigmoid * (1.0 + values * (1.0 - sigmoid))


def last_place(matches, places):
    return jnp.max(jnp.where(matches, places, 0), axis=0, keepdims=True)


def build_tables(mask, regrown, last_step, step_now, places, factors, sources, local_rows):
    columns, rows = mask.shape[1:]
    width = places.shape[1]
    right_bits = (2 * columns - 1).bit_length()
    left_bits = (2 * rows - 1).bit_length()

    def row_source(row):
        source = jnp.zeros_like(row)
        for at in range(1, sources):
            source += jnp.where(row >= at * local_rows, 1, 0)
        return source

    row = lax.broadcasted_iota(jnp.int32, (1, rows), 1)
    source = row_source(row)
    before = lax.broadcasted_iota(jnp.int32, (rows, rows), 0)
    after = lax.broadcasted_iota(jnp.int32, (rows, rows), 1)
    slots = lax.broadcasted_iota(jnp.int32, (width, rows), 0)
    codes = jnp.zeros((width, rows), jnp.int32)
    base = jnp.zeros((1, 1), jnp.int32)
    for matrix in range(2):
        counts = jnp.sum(mask[matrix], axis=0, keepdims=True)
        spread = jnp.broadcast_to(counts, (rows, rows)).T
        running = base + jnp.sum(jnp.where(before < after, spread, 0), axis=0, keepdims=True)
        left_code = (row + (source + matrix) * local_rows) << right_bits
        for column in range(columns):
            flag = mask[matrix, column : column + 1, :]
            state = (
                1
                + 2 * regrown[matrix, column : column + 1, :]
                + 4 * last_step[matrix, column : column + 1, :]
            )
            code = matrix * columns + column + left_code + (state << (right_bits + left_bits))
            wanted = jnp.where(flag == 1, running, -1)
            codes += jnp.where(slots == wanted, code, 0)
            running += flag
        base += jnp.sum(counts, axis=1, keepdims=True)

    def fields(code):
        state = code >> (right_bits + left_bits)
        right = code & ((1 << right_bits) - 1)
        left = (code >> right_bits) & ((1 << left_bits) - 1)
        return right, left, state & 1, (state >> 1) & 1, state >> 2

    right, left, live, fresh, last = fields(jnp.sum(codes.T, axis=0, keepdims=True))
    right_down, left_down, live_down, fresh_down, _ = fields(
        jnp.sum(codes, axis=1, keepdims=True)
    )
    usable = (live_down == 1) & (fresh_down == 0)
    column_key = jnp.where(usable, right_down, -1)
    row_key = jnp.where(usable & (right_down < columns), left_down, -1)
    down = lax.broadcasted_iota(jnp.int32, (width, width), 0)
    across = lax.broadcasted_iota(jnp.int32, (width, width), 1)
    place = down + 1
    earlier = down < across
    lane = lax.broadcasted_iota(jnp.int32, (1, width), 1)
    lane_left = lane + row_source(lane) * local_rows
    places[0:1, :] = left
    places[1:2, :] = right
    places[2:3, :] = last_place((column_key == right) & earlier, place)
    places[3:4, :] = last_place((row_key == left) & earlier, place)
    places[4:5, :] = last_place(column_key == lane, place)
    places[5:6, :] = last_place(row_key == lane_left, place)
    places[6:7, :] = live
    places[7:8, :] = fresh
    step = step_now[0]
    skipped = (step - last - 1).astype(jnp.float32)
    count = jnp.where(fresh == 1, 1, step).astype(jnp.float32)
    for at, beta in ((0, beta_one), (2, beta_two)):
        kept = beta * jnp.exp(skipped * math.log(beta))
        factors[at : at + 1, :] = jnp.where(fresh == 1, 0.0, kept)
        factors[at + 1 : at + 2, :] = 1.0 / (1.0 - jnp.exp(count * math.log(beta)))


LEFT, RIGHT, COLUMN_BEFORE, ROW_BEFORE, COLUMN_LAST, ROW_LAST, LIVE, FRESH = range(8)


INNER = 2
UNROLL = 8


def piece(index, chunk, chunks, shard):
    size = shard // chunks
    return pl.ds((index * chunks + chunk) * size, size)


def remote(src, dst, send_sem, recv_sem, axis, target):
    return pltpu.make_async_remote_copy(
        src_ref=src,
        dst_ref=dst,
        send_sem=send_sem,
        recv_sem=recv_sem,
        device_id={axis: target},
        device_id_type=pl.DeviceIdType.MESH,
    )


def greet(targets, meanwhile):
    barrier = pltpu.get_barrier_semaphore()
    for axis, target in targets:
        pl.semaphore_signal(
            barrier, inc=1, device_id={axis: target}, device_id_type=pl.DeviceIdType.MESH
        )
    meanwhile()
    pl.semaphore_wait(barrier, len(targets))


class LineGather:
    def __init__(self, axis, size, chunks, shard, out, sems):
        self.axis, self.chunks, self.out = axis, chunks, out
        self.recv, self.up, self.down, self.across = sems
        self.outer = size // INNER
        me = lax.axis_index(axis)
        self.me, self.mine, self.inner = me, me // INNER, me % INNER
        self.shard = shard

    def copy(self, source, chunk, way, inner=None):
        inner = self.inner if inner is None else inner
        index = source * INNER + inner
        at = self.out.at[piece(index, chunk, self.chunks, self.shard)]
        slot = source * self.chunks + chunk
        sem, target = {
            "up": (self.up, self.me + INNER),
            "down": (self.down, self.me - INNER),
            "across": (self.across, self.mine * INNER + 1 - self.inner),
        }[way]
        recv = self.recv.at[index * self.chunks + chunk]
        return remote(at, at, sem.at[slot], recv, self.axis, target)

    def wait_recv(self, source, chunk, inner):
        self.copy(source, chunk, "across", inner).wait_recv()

    def begin(self, chunk):
        mine = self.mine

        @pl.when(mine + 1 < self.outer)
        def _():
            self.copy(mine, chunk, "up").start()

        @pl.when(mine > 0)
        def _():
            self.copy(mine, chunk, "down").start()

        self.copy(mine, chunk, "across").start()

    def step(self, distance, chunk):
        low, high = self.mine - distance, self.mine + distance

        @pl.when(low >= 0)
        def _():
            self.wait_recv(low, chunk, self.inner)

            @pl.when(self.mine + 1 < self.outer)
            def _():
                self.copy(low, chunk, "up").start()

            self.copy(low, chunk, "across").start()

        @pl.when(high < self.outer)
        def _():
            self.wait_recv(high, chunk, self.inner)

            @pl.when(self.mine > 0)
            def _():
                self.copy(high, chunk, "down").start()

            self.copy(high, chunk, "across").start()

    def arrive(self, source):
        for chunk in range(self.chunks):
            self.wait_recv(source, chunk, 1 - self.inner)

    def finish(self):
        for source in range(self.outer):
            for chunk in range(self.chunks):
                self.copy(source, chunk, "across").wait_send()

                @pl.when((self.mine >= source) & (self.mine + 1 < self.outer))
                def _(source=source, chunk=chunk):
                    self.copy(source, chunk, "up").wait_send()

                @pl.when((self.mine <= source) & (self.mine > 0))
                def _(source=source, chunk=chunk):
                    self.copy(source, chunk, "down").wait_send()


class PairReduce:
    def __init__(self, axis, size, chunks, data, shard, near, far, sems):
        self.axis, self.chunks, self.data = axis, chunks, data
        self.near, self.far = near, far
        self.near_send, self.near_recv, self.far_send, self.far_recv = sems
        self.outer = size // INNER
        me = lax.axis_index(axis)
        self.me, self.mine, self.inner = me, me // INNER, me % INNER
        self.shard = shard
        self.size = shard // chunks

    def owner(self, offset):
        return lax.rem(self.mine + offset, self.outer)

    def targets(self):
        far = [
            (self.axis, self.owner(offset) * INNER + self.inner)
            for offset in range(1, self.outer)
        ]
        return far + [(self.axis, self.mine * INNER + 1 - self.inner)]

    def first(self, offset, chunk, inner):
        return ((self.owner(offset) * INNER + inner) * self.chunks + chunk) * self.size

    def near_copy(self, offset, chunk):
        owner = self.owner(offset)
        other = 1 - self.inner
        slot = owner * self.chunks + chunk
        return remote(
            self.data.at[piece(owner * INNER + other, chunk, self.chunks, self.shard)],
            self.near.at[piece(owner, chunk, self.chunks, self.shard)],
            self.near_send.at[slot],
            self.near_recv.at[slot],
            self.axis,
            self.mine * INNER + other,
        )

    def far_copy(self, offset, chunk):
        owner = self.owner(offset)
        return remote(
            self.near.at[piece(owner, chunk, self.chunks, self.shard)],
            self.far.at[piece(offset - 1, chunk, self.chunks, self.shard)],
            self.far_send.at[(offset - 1) * self.chunks + chunk],
            self.far_recv.at[(offset - 1) * self.chunks + chunk],
            self.axis,
            owner * INNER + self.inner,
        )

    def send_pair(self, offset, chunk):
        self.near_copy(offset, chunk).wait_recv()
        near_at = (self.owner(offset) * self.chunks + chunk) * self.size
        data_at = self.first(offset, chunk, self.inner)

        def add(index, carry):
            total = self.near[near_at + index].astype(jnp.float32)
            total += self.data[data_at + index].astype(jnp.float32)
            self.near[near_at + index] = total.astype(jnp.bfloat16)
            return carry

        lax.fori_loop(0, self.size, add, 0)
        self.far_copy(offset, chunk).start()

    def total(self, chunk, store):
        self.near_copy(0, chunk).wait_recv()
        for offset in range(1, self.outer):
            self.far_copy(offset, chunk).wait_recv()
        size = self.size
        near_at = (self.mine * self.chunks + chunk) * size
        data_at = (self.me * self.chunks + chunk) * size

        def add(index, carry):
            total = self.near[near_at + index].astype(jnp.float32)
            total += self.data[data_at + index].astype(jnp.float32)
            for offset in range(1, self.outer):
                at = ((offset - 1) * self.chunks + chunk) * size
                total += self.far[at + index].astype(jnp.float32)
            store(chunk * size + index, total)
            return carry

        lax.fori_loop(0, size, add, 0)

    def finish(self):
        for chunk in range(self.chunks):
            for offset in range(self.outer):
                self.near_copy(offset, chunk).wait_send()
                if offset > 0:
                    self.far_copy(offset, chunk).wait_send()


def chain_products(count, product, chain, table, previous):
    unroll = math.gcd(UNROLL, count)

    def step(index, carry):
        base = index * unroll
        parts = [product(base + k) for k in range(unroll)]
        for k in range(unroll):
            chain[base + k + 1] = parts[k] + chain[table[previous, base + k]]
        return carry

    lax.fori_loop(0, count // unroll, step, 0)


def make_tiles(table, left_ref, right_ref, tiles_ref, first, count, scale):
    unroll = math.gcd(UNROLL, count)

    def step(index, carry):
        base = first + index * unroll
        for k in range(unroll):
            tile = lax.dot_general(
                left_ref[table[LEFT, base + k]],
                right_ref[table[RIGHT, base + k]],
                (((0,), (0,)), ((), ())),
                preferred_element_type=jnp.float32,
            )
            tiles_ref[base + k] = (scale * tile).astype(jnp.bfloat16)
        return carry

    lax.fori_loop(0, count // unroll, step, 0)


def step_kernel(
    sizes,
    gather_chunks,
    reduce_chunks,
    scale,
    weights,
    first_in,
    second_in,
    tokens,
    grad_out,
    mask,
    regrown,
    last_step,
    step_now,
    rows_out,
    new_weights,
    new_first,
    new_second,
    packed,
    left,
    chain,
    right,
    tiles,
    rows,
    wide_near,
    wide_far,
    thin_near,
    thin_far,
    places,
    factors,
    table,
    factor,
    *sems,
):
    local, sems = sems[:3], sems[3:]
    owned, side = new_weights.shape[0], new_weights.shape[1]
    slot_total, columns, row_blocks = packed.shape[0], right.shape[0] // 2, rows.shape[0]
    local_rows = rows_out.shape[1] // side
    line = LineGather("dp", sizes[0], gather_chunks[0], owned, packed, sems[:4])
    wing = LineGather("tensor", sizes[1], gather_chunks[1], 2 * local_rows, left, sems[4:8])
    wide = PairReduce(
        "dp", sizes[0], reduce_chunks[0], tiles, owned, wide_near, wide_far, sems[8:12]
    )
    thin = PairReduce(
        "tensor", sizes[1], reduce_chunks[1], rows, local_rows, thin_near, thin_far, sems[12:]
    )

    def load_left(index):
        source = tokens if index < local_rows else grad_out
        return pltpu.make_async_copy(
            source.at[:, pl.ds(index % local_rows * side, side)],
            left.at[wing.me * 2 * local_rows + index],
            local[0].at[index],
        )

    def load_weights(chunk):
        at = piece(0, chunk, line.chunks, owned)
        return pltpu.make_async_copy(weights.at[at], new_weights.at[at], local[1].at[chunk])

    def round_weights(chunk):
        load_weights(chunk).wait()
        size = owned // line.chunks
        at = chunk * size
        mine = line.me * owned + at

        def round_block(index, carry):
            packed[mine + index] = new_weights[at + index].astype(jnp.bfloat16)
            return carry

        lax.fori_loop(0, size, round_block, 0)

    moments = [
        pltpu.make_async_copy(first_in, new_first, local[2].at[0]),
        pltpu.make_async_copy(second_in, new_second, local[2].at[1]),
    ]
    load_tables = [
        pltpu.make_async_copy(places, table, local[2].at[2]),
        pltpu.make_async_copy(factors, factor, local[2].at[3]),
    ]

    def meanwhile():
        load_weights(0).start()
        for index in range(2 * local_rows):
            load_left(index).start()
        for chunk in range(1, line.chunks):
            load_weights(chunk).start()
        round_weights(0)
        for index in range(2 * local_rows):
            load_left(index).wait()

    greet(wide.targets() + thin.targets(), meanwhile)
    line.begin(0)
    for chunk in range(wing.chunks):
        wing.begin(chunk)
    for chunk in range(1, line.chunks):
        round_weights(chunk)
        line.begin(chunk)
    for copy in moments:
        copy.start()
    chain[0] = jnp.zeros(chain.shape[1:], jnp.float32)
    build_tables(
        mask, regrown, last_step, step_now, places, factors, sizes[1], local_rows
    )
    for copy in load_tables:
        copy.start()

    events = []
    for gather, weight in ((line, 1.5), (wing, 1.0)):
        for chunk in range(gather.chunks):
            for distance in range(1, gather.outer):
                passed = (distance - 1 + (chunk + 1) / gather.chunks) / (gather.outer - 1)
                events.append((weight * passed, gather, distance, chunk))
    events.sort(key=lambda event: event[0])
    for _, gather, distance, chunk in events:
        gather.step(distance, chunk)
    for copy in load_tables:
        copy.wait()
    for source in range(wing.outer):
        wing.arrive(source)
    for source in range(line.outer):
        line.arrive(source)

    def forward(slot):
        return jnp.dot(
            left[table[LEFT, slot]], packed[slot], preferred_element_type=jnp.float32
        )

    chain_products(slot_total, forward, chain, table, COLUMN_BEFORE)

    def activate(column, carry):
        pre_act = scale * chain[table[COLUMN_LAST, column]]
        back_act = scale * chain[table[COLUMN_LAST, columns + column]]
        right[column] = (back_act * silu_slope(pre_act)).astype(jnp.bfloat16)
        right[columns + column] = jax.nn.silu(pre_act).astype(jnp.bfloat16)
        return carry

    lax.fori_loop(0, columns, activate, 0)

    def backward(slot):
        return lax.dot_general(
            right[table[RIGHT, slot]],
            packed[slot],
            (((1,), (1,)), ((), ())),
            preferred_element_type=jnp.float32,
        )

    def sum_rows():
        chain_products(slot_total, backward, chain, table, ROW_BEFORE)

        def finish(index, carry):
            rows[index] = (scale * chain[table[ROW_LAST, index]]).astype(jnp.bfloat16)
            return carry

        lax.fori_loop(0, row_blocks, finish, 0)
        for offset in list(range(1, thin.outer)) + [0]:
            for chunk in range(thin.chunks):
                thin.near_copy(offset, chunk).start()

    def tiles_of(offset, chunk, inner):
        first = wide.first(offset, chunk, inner)
        make_tiles(table, left, right, tiles, first, wide.size, scale)

    def update(index, gradient):
        slot = wide.me * owned + index
        live = table[LIVE, slot] == 1
        weight, first, second = new_weights[index], new_first[index], new_second[index]
        mean = factor[0, slot] * first + (1.0 - beta_one) * gradient
        square = factor[2, slot] * second + (1.0 - beta_two) * gradient * gradient
        spread = jnp.sqrt(factor[3, slot] * square) + epsilon
        base = jnp.where(table[FRESH, slot] == 1, 0.0, weight)
        moved = (1.0 - learn_rate * decay_rate) * base
        moved -= learn_rate * (factor[1, slot] * mean / spread)
        new_weights[index] = jnp.where(live, moved, weight)
        new_first[index] = jnp.where(live, mean, first)
        new_second[index] = jnp.where(live, square, second)

    def store_row(index, total):
        at = pl.ds(pl.multiple_of(index * side, side), side)
        rows_out[:, at] = total.astype(jnp.bfloat16)

    far_steps = [(o, k) for o in range(1, wide.outer) for k in range(wide.chunks)]
    last_far = len(far_steps) - 1
    for at, step in enumerate(far_steps):
        tiles_of(*step, 1 - wide.inner)
        wide.near_copy(*step).start()
        if at > 0:
            wide.send_pair(*far_steps[at - 1])
        tiles_of(*step, wide.inner)
        if at == min(2, last_far):
            sum_rows()
    wide.send_pair(*far_steps[-1])
    thin_pairs = [(o, k) for o in range(1, thin.outer) for k in range(thin.chunks)]
    for chunk in range(wide.chunks):
        tiles_of(0, chunk, 1 - wide.inner)
        wide.near_copy(0, chunk).start()
        tiles_of(0, chunk, wide.inner)
        low = chunk * len(thin_pairs) // wide.chunks
        high = (chunk + 1) * len(thin_pairs) // wide.chunks
        for pair in thin_pairs[low:high]:
            thin.send_pair(*pair)
    for copy in moments:
        copy.wait()
    for chunk in range(wide.chunks - 1):
        wide.total(chunk, update)
    for chunk in range(thin.chunks):
        thin.total(chunk, store_row)
    line.finish()
    wing.finish()
    wide.total(wide.chunks - 1, update)
    wide.finish()
    thin.finish()


def run_step(
    weights, first, second, tokens, grad_out, mask, regrown, last_step, step_now, scale
):
    sizes = (lax.axis_size("dp"), lax.axis_size("tensor"))
    owned, side = weights.shape[0], weights.shape[1]
    tok_count = tokens.shape[0]
    local_rows = tokens.shape[1] // side
    columns, row_blocks = mask.shape[1:]
    slot_total = owned * sizes[0]
    outer = [size // INNER for size in sizes]
    gather_chunks = (math.gcd(8, owned), math.gcd(4, 2 * local_rows))
    reduce_chunks = (math.gcd(8, owned), math.gcd(2, local_rows))
    block = (tok_count, side)
    tile = (side, side)
    dma = pltpu.SemaphoreType.DMA
    width = -(-max(slot_total, row_blocks, 2 * columns) // 128) * 128

    def scratch(count, shape, kind=jnp.bfloat16):
        return pltpu.VMEM((count,) + shape, kind)

    shapes = [
        scratch(slot_total, tile),
        scratch(2 * local_rows * sizes[1], block),
        scratch(slot_total + 1, block, jnp.float32),
        scratch(2 * columns, block),
        scratch(slot_total, tile),
        scratch(row_blocks, block),
        scratch(outer[0] * owned, tile),
        scratch(max(outer[0] - 1, 1) * owned, tile),
        scratch(outer[1] * local_rows, block),
        scratch(max(outer[1] - 1, 1) * local_rows, block),
        pltpu.VMEM((8, width), jnp.int32),
        pltpu.VMEM((8, width), jnp.float32),
        pltpu.SMEM((8, width), jnp.int32),
        pltpu.SMEM((8, width), jnp.float32),
        dma((2 * local_rows,)),
        dma((gather_chunks[0],)),
        dma((4,)),
    ]
    for size, chunks in zip(sizes, gather_chunks):
        shapes += [dma((size * chunks,))] + [dma((size // INNER * chunks,))] * 3
    for count, chunks in zip(outer, reduce_chunks):
        shapes += [dma((count * chunks,))] * 2 + [dma((max(count - 1, 1) * chunks,))] * 2
    vmem = pl.BlockSpec(memory_space=pltpu.VMEM)
    smem = pl.BlockSpec(memory_space=pltpu.SMEM)
    anywhere = pl.BlockSpec(memory_space=pl.ANY)
    return pl.pallas_call(
        functools.partial(step_kernel, sizes, gather_chunks, reduce_chunks, scale),
        out_shape=(pltpu.VMEM(tokens.shape, jnp.bfloat16),)
        + (pltpu.VMEM((owned,) + tile, jnp.float32),) * 3,
        in_specs=[anywhere] * 5 + [vmem] * 3 + [smem],
        out_specs=(vmem,) * 4,
        scratch_shapes=shapes,
        compiler_params=pltpu.CompilerParams(
            collective_id=0, has_side_effects=True, vmem_limit_bytes=49 * 1024 * 1024
        ),
    )(weights, first, second, tokens, grad_out, mask, regrown, last_step, step_now)


def per_device(
    tokens,
    grad_out,
    packed_weight_blocks,
    packed_first_moments,
    packed_second_moments,
    block_mask,
    last_step,
    regrown,
    step_now,
):
    scale_factor = 3.0 / math.sqrt(D)
    mask, fresh, last = (grid.transpose(0, 2, 1) for grid in (block_mask, regrown, last_step))
    return run_step(
        packed_weight_blocks,
        packed_first_moments,
        packed_second_moments,
        tokens,
        grad_out,
        mask,
        fresh,
        last,
        step_now,
        scale_factor,
    )


def solution(mesh):
    in_specs = (
        P("dp", "tensor"),
        P("dp", "tensor"),
        P(("dp", "tensor"), None, None),
        P(("dp", "tensor"), None, None),
        P(("dp", "tensor"), None, None),
        P(None, None, "tensor"),
        P(None, None, "tensor"),
        P(None, None, "tensor"),
        P(),
    )
    out_specs = (
        P("dp", "tensor"),
        P(("dp", "tensor"), None, None),
        P(("dp", "tensor"), None, None),
        P(("dp", "tensor"), None, None),
    )
    return jax.shard_map(
        per_device, mesh=mesh, in_specs=in_specs, out_specs=out_specs, check_vma=False
    )
```

```python
import functools
import math

import jax
import jax.numpy as jnp
from jax import lax
from jax.experimental import pallas as pl
from jax.experimental.pallas import tpu as pltpu
from jax.sharding import PartitionSpec as P

D = 8192


beta_one = 0.9
beta_two = 0.95
learn_rate = 0.05
decay_rate = 0.1
epsilon = 0.05


def silu_slope(values):
    sigmoid = jax.nn.sigmoid(values)
    return sigmoid * (1.0 + values * (1.0 - sigmoid))


def last_place(matches, places):
    return jnp.max(jnp.where(matches, places, 0), axis=0, keepdims=True)


def build_tables(
    mask, regrown, last_step, step_now, places, factors, sources, local_rows, order
):
    columns, rows = mask.shape[1:]
    width = places.shape[1]
    right_bits = (2 * columns - 1).bit_length()
    left_bits = (2 * rows - 1).bit_length()

    def row_source(row):
        source = jnp.zeros_like(row)
        for at in range(1, sources):
            source += jnp.where(row >= at * local_rows, 1, 0)
        return source

    row = lax.broadcasted_iota(jnp.int32, (1, rows), 1)
    source = row_source(row)
    before = lax.broadcasted_iota(jnp.int32, (rows, rows), 0)
    after = lax.broadcasted_iota(jnp.int32, (rows, rows), 1)
    slots = lax.broadcasted_iota(jnp.int32, (width, rows), 0)
    codes = jnp.zeros((width, rows), jnp.int32)
    base = jnp.zeros((1, 1), jnp.int32)
    for matrix in range(2):
        counts = jnp.sum(mask[matrix], axis=0, keepdims=True)
        spread = jnp.broadcast_to(counts, (rows, rows)).T
        running = base + jnp.sum(jnp.where(before < after, spread, 0), axis=0, keepdims=True)
        left_code = (row + (source + matrix) * local_rows) << right_bits
        for column in range(columns):
            flag = mask[matrix, column : column + 1, :]
            state = (
                1
                + 2 * regrown[matrix, column : column + 1, :]
                + 4 * last_step[matrix, column : column + 1, :]
            )
            code = matrix * columns + column + left_code + (state << (right_bits + left_bits))
            wanted = jnp.where(flag == 1, running, -1)
            codes += jnp.where(slots == wanted, code, 0)
            running += flag
        base += jnp.sum(counts, axis=1, keepdims=True)

    def fields(code):
        state = code >> (right_bits + left_bits)
        right = code & ((1 << right_bits) - 1)
        left = (code >> right_bits) & ((1 << left_bits) - 1)
        return right, left, state & 1, (state >> 1) & 1, state >> 2

    right, left, live, fresh, last = fields(jnp.sum(codes.T, axis=0, keepdims=True))
    right_down, left_down, live_down, fresh_down, _ = fields(
        jnp.sum(codes, axis=1, keepdims=True)
    )
    usable = (live_down == 1) & (fresh_down == 0)
    column_key = jnp.where(usable, right_down, -1)
    row_key = jnp.where(usable & (right_down < columns), left_down, -1)
    down = lax.broadcasted_iota(jnp.int32, (width, 1), 0)
    across = lax.broadcasted_iota(jnp.int32, (1, width), 1)
    earlier = order(down) < order(across)
    place = order(down) + 1
    lane = lax.broadcasted_iota(jnp.int32, (1, width), 1)
    lane_left = lane + row_source(lane) * local_rows
    places[0:1, :] = left
    places[1:2, :] = right
    places[2:3, :] = last_place((column_key == right) & earlier, place)
    places[3:4, :] = last_place((row_key == left) & (down < across), down + 1)
    places[4:5, :] = last_place(column_key == lane, place)
    places[5:6, :] = last_place(row_key == lane_left, down + 1)
    places[6:7, :] = live
    places[7:8, :] = fresh
    step = step_now[0]
    skipped = (step - last - 1).astype(jnp.float32)
    count = jnp.where(fresh == 1, 1, step).astype(jnp.float32)
    for at, beta in ((0, beta_one), (2, beta_two)):
        kept = beta * jnp.exp(skipped * math.log(beta))
        factors[at : at + 1, :] = jnp.where(fresh == 1, 0.0, kept)
        factors[at + 1 : at + 2, :] = 1.0 / (1.0 - jnp.exp(count * math.log(beta)))


LEFT, RIGHT, COLUMN_BEFORE, ROW_BEFORE, COLUMN_LAST, ROW_LAST, LIVE, FRESH = range(8)


INNER = 2
UNROLL = 8


def piece(index, chunk, chunks, shard):
    size = shard // chunks
    return pl.ds((index * chunks + chunk) * size, size)


def remote(src, dst, send_sem, recv_sem, axis, target):
    return pltpu.make_async_remote_copy(
        src_ref=src,
        dst_ref=dst,
        send_sem=send_sem,
        recv_sem=recv_sem,
        device_id={axis: target},
        device_id_type=pl.DeviceIdType.MESH,
    )


def greet(targets, meanwhile):
    barrier = pltpu.get_barrier_semaphore()
    for axis, target in targets:
        pl.semaphore_signal(
            barrier, inc=1, device_id={axis: target}, device_id_type=pl.DeviceIdType.MESH
        )
    meanwhile()
    pl.semaphore_wait(barrier, len(targets))


class LineGather:
    def __init__(self, axis, size, chunks, shard, out, sems, balanced=False):
        self.axis, self.chunks, self.out = axis, chunks, out
        self.recv, self.up, self.down, self.across, self.pass_up, self.pass_down = sems
        self.balanced = balanced
        self.outer = size // INNER
        me = lax.axis_index(axis)
        self.me, self.mine, self.inner = me, me // INNER, me % INNER
        self.shard = shard

    def copy(self, source, chunk, way, inner=None):
        inner = self.inner if inner is None else inner
        index = source * INNER + inner
        at = self.out.at[piece(index, chunk, self.chunks, self.shard)]
        slot = source * self.chunks + chunk
        sem, target = {
            "up": (self.up, self.me + INNER),
            "down": (self.down, self.me - INNER),
            "across": (self.across, self.mine * INNER + 1 - self.inner),
            "pass_up": (self.pass_up, self.me + INNER),
            "pass_down": (self.pass_down, self.me - INNER),
        }[way]
        recv = self.recv.at[index * self.chunks + chunk]
        return remote(at, at, sem.at[slot], recv, self.axis, target)

    def wait_recv(self, source, chunk, inner):
        self.copy(source, chunk, "across", inner).wait_recv()

    def begin(self, chunk):
        mine = self.mine

        @pl.when(mine + 1 < self.outer)
        def _():
            self.copy(mine, chunk, "up").start()

        @pl.when(mine > 0)
        def _():
            self.copy(mine, chunk, "down").start()

        self.copy(mine, chunk, "across").start()

    def passed(self, chunk):
        return self.balanced and chunk % 2 == 1

    def pass_on(self, chunk):
        other = 1 - self.inner
        self.wait_recv(self.mine, chunk, other)

        @pl.when(self.mine + 1 < self.outer)
        def _():
            self.copy(self.mine, chunk, "pass_up", other).start()

        @pl.when(self.mine > 0)
        def _():
            self.copy(self.mine, chunk, "pass_down", other).start()

    def step(self, distance, chunk):
        low, high = self.mine - distance, self.mine + distance
        crosses = distance > 1 or not self.passed(chunk)

        @pl.when(low >= 0)
        def _():
            self.wait_recv(low, chunk, self.inner)

            @pl.when(self.mine + 1 < self.outer)
            def _():
                self.copy(low, chunk, "up").start()

            if crosses:
                self.copy(low, chunk, "across").start()

        @pl.when(high < self.outer)
        def _():
            self.wait_recv(high, chunk, self.inner)

            @pl.when(self.mine > 0)
            def _():
                self.copy(high, chunk, "down").start()

            if crosses:
                self.copy(high, chunk, "across").start()

    def arrive(self, source):
        for chunk in range(self.chunks):
            if self.passed(chunk):

                @pl.when(self.mine != source)
                def _(chunk=chunk):
                    self.wait_recv(source, chunk, 1 - self.inner)

            else:
                self.wait_recv(source, chunk, 1 - self.inner)

    def finish(self):
        for source in range(self.outer):
            for chunk in range(self.chunks):
                if self.passed(chunk):

                    @pl.when((self.mine != source + 1) & (self.mine + 1 != source))
                    def _(source=source, chunk=chunk):
                        self.copy(source, chunk, "across").wait_send()

                    @pl.when((self.mine == source) & (self.mine + 1 < self.outer))
                    def _(source=source, chunk=chunk):
                        self.copy(source, chunk, "pass_up", 1 - self.inner).wait_send()

                    @pl.when((self.mine == source) & (self.mine > 0))
                    def _(source=source, chunk=chunk):
                        self.copy(source, chunk, "pass_down", 1 - self.inner).wait_send()

                else:
                    self.copy(source, chunk, "across").wait_send()

                @pl.when((self.mine >= source) & (self.mine + 1 < self.outer))
                def _(source=source, chunk=chunk):
                    self.copy(source, chunk, "up").wait_send()

                @pl.when((self.mine <= source) & (self.mine > 0))
                def _(source=source, chunk=chunk):
                    self.copy(source, chunk, "down").wait_send()


class PairReduce:
    def __init__(self, axis, size, chunks, data, shard, near, far, sems):
        self.axis, self.chunks, self.data = axis, chunks, data
        self.near, self.far = near, far
        self.near_send, self.near_recv, self.far_send, self.far_recv = sems
        self.outer = size // INNER
        me = lax.axis_index(axis)
        self.me, self.mine, self.inner = me, me // INNER, me % INNER
        self.shard = shard
        self.size = shard // chunks

    def owner(self, offset):
        return lax.rem(self.mine + offset, self.outer)

    def targets(self):
        far = [
            (self.axis, self.owner(offset) * INNER + self.inner)
            for offset in range(1, self.outer)
        ]
        return far + [(self.axis, self.mine * INNER + 1 - self.inner)]

    def first(self, offset, chunk, inner):
        return ((self.owner(offset) * INNER + inner) * self.chunks + chunk) * self.size

    def near_copy(self, offset, chunk):
        owner = self.owner(offset)
        other = 1 - self.inner
        slot = owner * self.chunks + chunk
        return remote(
            self.data.at[piece(owner * INNER + other, chunk, self.chunks, self.shard)],
            self.near.at[piece(owner, chunk, self.chunks, self.shard)],
            self.near_send.at[slot],
            self.near_recv.at[slot],
            self.axis,
            self.mine * INNER + other,
        )

    def far_copy(self, offset, chunk):
        owner = self.owner(offset)
        return remote(
            self.near.at[piece(owner, chunk, self.chunks, self.shard)],
            self.far.at[piece(offset - 1, chunk, self.chunks, self.shard)],
            self.far_send.at[(offset - 1) * self.chunks + chunk],
            self.far_recv.at[(offset - 1) * self.chunks + chunk],
            self.axis,
            owner * INNER + self.inner,
        )

    def send_pair(self, offset, chunk):
        self.near_copy(offset, chunk).wait_recv()
        near_at = (self.owner(offset) * self.chunks + chunk) * self.size
        data_at = self.first(offset, chunk, self.inner)

        def add(index, carry):
            total = self.near[near_at + index].astype(jnp.float32)
            total += self.data[data_at + index].astype(jnp.float32)
            self.near[near_at + index] = total.astype(jnp.bfloat16)
            return carry

        lax.fori_loop(0, self.size, add, 0)
        self.far_copy(offset, chunk).start()

    def total(self, chunk, store):
        self.near_copy(0, chunk).wait_recv()
        for offset in range(1, self.outer):
            self.far_copy(offset, chunk).wait_recv()
        size = self.size
        near_at = (self.mine * self.chunks + chunk) * size
        data_at = (self.me * self.chunks + chunk) * size

        def add(index, carry):
            total = self.near[near_at + index].astype(jnp.float32)
            total += self.data[data_at + index].astype(jnp.float32)
            for offset in range(1, self.outer):
                at = ((offset - 1) * self.chunks + chunk) * size
                total += self.far[at + index].astype(jnp.float32)
            store(chunk * size + index, total)
            return carry

        lax.fori_loop(0, size, add, 0)

    def finish(self):
        for chunk in range(self.chunks):
            for offset in range(self.outer):
                self.near_copy(offset, chunk).wait_send()
                if offset > 0:
                    self.far_copy(offset, chunk).wait_send()


def chain_products(count, product, chain, table, previous, slot, place):
    unroll = math.gcd(UNROLL, count)

    def step(index, carry):
        base = index * unroll
        parts = [product(slot + base + k) for k in range(unroll)]
        for k in range(unroll):
            before = table[previous, slot + base + k]
            chain[place + base + k + 1] = parts[k] + chain[before]
        return carry

    lax.fori_loop(0, count // unroll, step, 0)


def make_tiles(table, left_ref, right_ref, tiles_ref, first, count, scale):
    unroll = math.gcd(UNROLL, count)

    def step(index, carry):
        base = first + index * unroll
        for k in range(unroll):
            tile = lax.dot_general(
                left_ref[table[LEFT, base + k]],
                right_ref[table[RIGHT, base + k]],
                (((0,), (0,)), ((), ())),
                preferred_element_type=jnp.float32,
            )
            tiles_ref[base + k] = (scale * tile).astype(jnp.bfloat16)
        return carry

    lax.fori_loop(0, count // unroll, step, 0)


def step_kernel(
    sizes,
    gather_chunks,
    reduce_chunks,
    scale,
    weights,
    first_in,
    second_in,
    tokens,
    grad_out,
    mask,
    regrown,
    last_step,
    step_now,
    rows_out,
    new_weights,
    new_first,
    new_second,
    packed,
    left,
    chain,
    right,
    tiles,
    rows,
    wide_near,
    wide_far,
    thin_near,
    thin_far,
    places,
    factors,
    table,
    factor,
    *sems,
):
    local, sems = sems[:3], sems[3:]
    owned, side = new_weights.shape[0], new_weights.shape[1]
    slot_total, columns, row_blocks = packed.shape[0], right.shape[0] // 2, rows.shape[0]
    local_rows = rows_out.shape[1] // side
    line = LineGather("dp", sizes[0], gather_chunks[0], owned, packed, sems[:6])
    wing = LineGather(
        "tensor", sizes[1], gather_chunks[1], 2 * local_rows, left, sems[6:12], True
    )
    wide = PairReduce(
        "dp", sizes[0], reduce_chunks[0], tiles, owned, wide_near, wide_far, sems[12:16]
    )
    thin = PairReduce(
        "tensor", sizes[1], reduce_chunks[1], rows, local_rows, thin_near, thin_far, sems[16:]
    )

    def load_left(index):
        source = tokens if index < local_rows else grad_out
        return pltpu.make_async_copy(
            source.at[:, pl.ds(index % local_rows * side, side)],
            left.at[wing.me * 2 * local_rows + index],
            local[0].at[index],
        )

    def load_weights(chunk):
        at = piece(0, chunk, line.chunks, owned)
        return pltpu.make_async_copy(weights.at[at], new_weights.at[at], local[1].at[chunk])

    def round_weights(chunk):
        load_weights(chunk).wait()
        size = owned // line.chunks
        at = chunk * size
        mine = line.me * owned + at

        def round_block(index, carry):
            packed[mine + index] = new_weights[at + index].astype(jnp.bfloat16)
            return carry

        lax.fori_loop(0, size, round_block, 0)

    moments = [
        pltpu.make_async_copy(first_in, new_first, local[2].at[0]),
        pltpu.make_async_copy(second_in, new_second, local[2].at[1]),
    ]
    load_tables = [
        pltpu.make_async_copy(places, table, local[2].at[2]),
        pltpu.make_async_copy(factors, factor, local[2].at[3]),
    ]

    def meanwhile():
        load_weights(0).start()
        for index in range(2 * local_rows):
            load_left(index).start()
        for chunk in range(1, line.chunks):
            load_weights(chunk).start()
        round_weights(0)
        for index in range(2 * local_rows):
            load_left(index).wait()

    greet(wide.targets() + thin.targets(), meanwhile)
    line.begin(0)
    for chunk in range(wing.chunks):
        wing.begin(chunk)
    for chunk in range(1, line.chunks):
        round_weights(chunk)
        line.begin(chunk)
    for copy in moments:
        copy.start()
    chain[0] = jnp.zeros(chain.shape[1:], jnp.float32)
    size = owned // line.chunks

    def pair_at(offset):
        return lax.rem(line.mine + offset, line.outer)

    staged = line.outer == 2
    segments = []
    for offset in range(line.outer):
        first = pair_at(offset) * INNER * owned
        if offset == 0 or not staged:
            segments.append((offset, None, first, INNER * owned))
        else:
            for chunk in range(line.chunks):
                for inner in range(INNER):
                    at = first + inner * owned + chunk * size
                    segments.append((offset, chunk if inner == 0 else None, at, size))

    def order(slots):
        ordered, place = slots, 0
        for _, _, first, count in segments:
            inside = (slots >= first) & (slots < first + count)
            ordered = jnp.where(inside, slots - first + place, ordered)
            place += count
        return ordered

    build_tables(
        mask, regrown, last_step, step_now, places, factors, sizes[1], local_rows, order
    )
    for copy in load_tables:
        copy.start()

    events = []
    for gather, weight in ((line, 1.2), (wing, 1.0)):
        for chunk in range(gather.chunks):
            for distance in range(1, gather.outer):
                passed = (distance - 1 + (chunk + 1) / gather.chunks) / (gather.outer - 1)
                events.append((weight * passed, gather.step, (distance, chunk), gather is line))
            if gather.passed(chunk):
                passed = (chunk + 1) / gather.chunks / (gather.outer - 1)
                events.append((weight * passed, gather.pass_on, (chunk,), False))
    events.sort(key=lambda event: event[0])
    deferred = []
    for when, act, which, late in events:
        if late and when > 1.0:
            deferred.append((act, which))
        else:
            act(*which)
    for copy in load_tables:
        copy.wait()
    for source in range(wing.outer):
        wing.arrive(source)

    def forward(slot):
        return jnp.dot(
            left[table[LEFT, slot]], packed[slot], preferred_element_type=jnp.float32
        )

    if not staged:
        for act, which in deferred:
            act(*which)
        for offset in range(1, line.outer):
            line.arrive(pair_at(offset))
        deferred = []
    line.arrive(line.mine)
    place = 0
    for offset, chunk, first, count in segments:
        if chunk is not None:
            if deferred and deferred[0][1] == (offset, chunk):
                act, which = deferred.pop(0)
                act(*which)
            line.wait_recv(pair_at(offset), chunk, 1 - line.inner)
        chain_products(count, forward, chain, table, COLUMN_BEFORE, first, place)
        place += count

    def activate(column, carry):
        pre_act = scale * chain[table[COLUMN_LAST, column]]
        back_act = scale * chain[table[COLUMN_LAST, columns + column]]
        right[column] = (back_act * silu_slope(pre_act)).astype(jnp.bfloat16)
        right[columns + column] = jax.nn.silu(pre_act).astype(jnp.bfloat16)
        return carry

    lax.fori_loop(0, columns, activate, 0)

    def backward(slot):
        return lax.dot_general(
            right[table[RIGHT, slot]],
            packed[slot],
            (((1,), (1,)), ((), ())),
            preferred_element_type=jnp.float32,
        )

    def sum_rows():
        chain_products(slot_total, backward, chain, table, ROW_BEFORE, 0, 0)

        def finish(index, carry):
            rows[index] = (scale * chain[table[ROW_LAST, index]]).astype(jnp.bfloat16)
            return carry

        lax.fori_loop(0, row_blocks, finish, 0)
        for offset in list(range(1, thin.outer)) + [0]:
            for chunk in range(thin.chunks):
                thin.near_copy(offset, chunk).start()

    def tiles_of(offset, chunk, inner):
        first = wide.first(offset, chunk, inner)
        make_tiles(table, left, right, tiles, first, wide.size, scale)

    def update(index, gradient):
        slot = wide.me * owned + index
        live = table[LIVE, slot] == 1
        weight, first, second = new_weights[index], new_first[index], new_second[index]
        mean = factor[0, slot] * first + (1.0 - beta_one) * gradient
        square = factor[2, slot] * second + (1.0 - beta_two) * gradient * gradient
        spread = jnp.sqrt(factor[3, slot] * square) + epsilon
        base = jnp.where(table[FRESH, slot] == 1, 0.0, weight)
        moved = (1.0 - learn_rate * decay_rate) * base
        moved -= learn_rate * (factor[1, slot] * mean / spread)
        new_weights[index] = jnp.where(live, moved, weight)
        new_first[index] = jnp.where(live, mean, first)
        new_second[index] = jnp.where(live, square, second)

    def store_row(index, total):
        at = pl.ds(pl.multiple_of(index * side, side), side)
        rows_out[:, at] = total.astype(jnp.bfloat16)

    far_steps = [(o, k) for o in range(1, wide.outer) for k in range(wide.chunks)]
    last_far = len(far_steps) - 1
    for at, step in enumerate(far_steps):
        tiles_of(*step, 1 - wide.inner)
        wide.near_copy(*step).start()
        if at > 0:
            wide.send_pair(*far_steps[at - 1])
        tiles_of(*step, wide.inner)
        if at == min(2, last_far):
            sum_rows()
    wide.send_pair(*far_steps[-1])
    thin_pairs = [(o, k) for o in range(1, thin.outer) for k in range(thin.chunks)]
    for chunk in range(wide.chunks):
        tiles_of(0, chunk, 1 - wide.inner)
        wide.near_copy(0, chunk).start()
        tiles_of(0, chunk, wide.inner)
        low = chunk * len(thin_pairs) // wide.chunks
        high = (chunk + 1) * len(thin_pairs) // wide.chunks
        for pair in thin_pairs[low:high]:
            thin.send_pair(*pair)
    for copy in moments:
        copy.wait()
    for chunk in range(wide.chunks - 1):
        wide.total(chunk, update)
    for chunk in range(thin.chunks):
        thin.total(chunk, store_row)
    line.finish()
    wing.finish()
    wide.total(wide.chunks - 1, update)
    wide.finish()
    thin.finish()


def run_step(
    weights, first, second, tokens, grad_out, mask, regrown, last_step, step_now, scale
):
    sizes = (lax.axis_size("dp"), lax.axis_size("tensor"))
    owned, side = weights.shape[0], weights.shape[1]
    tok_count = tokens.shape[0]
    local_rows = tokens.shape[1] // side
    columns, row_blocks = mask.shape[1:]
    slot_total = owned * sizes[0]
    outer = [size // INNER for size in sizes]
    gather_chunks = (math.gcd(8, owned), math.gcd(4, 2 * local_rows))
    reduce_chunks = (math.gcd(8, owned), math.gcd(2, local_rows))
    block = (tok_count, side)
    tile = (side, side)
    dma = pltpu.SemaphoreType.DMA
    width = -(-max(slot_total, row_blocks, 2 * columns) // 128) * 128

    def scratch(count, shape, kind=jnp.bfloat16):
        return pltpu.VMEM((count,) + shape, kind)

    shapes = [
        scratch(slot_total, tile),
        scratch(2 * local_rows * sizes[1], block),
        scratch(slot_total + 1, block, jnp.float32),
        scratch(2 * columns, block),
        scratch(slot_total, tile),
        scratch(row_blocks, block),
        scratch(outer[0] * owned, tile),
        scratch(max(outer[0] - 1, 1) * owned, tile),
        scratch(outer[1] * local_rows, block),
        scratch(max(outer[1] - 1, 1) * local_rows, block),
        pltpu.VMEM((8, width), jnp.int32),
        pltpu.VMEM((8, width), jnp.float32),
        pltpu.SMEM((8, width), jnp.int32),
        pltpu.SMEM((8, width), jnp.float32),
        dma((2 * local_rows,)),
        dma((gather_chunks[0],)),
        dma((4,)),
    ]
    for size, chunks in zip(sizes, gather_chunks):
        shapes += [dma((size * chunks,))] + [dma((size // INNER * chunks,))] * 5
    for count, chunks in zip(outer, reduce_chunks):
        shapes += [dma((count * chunks,))] * 2 + [dma((max(count - 1, 1) * chunks,))] * 2
    vmem = pl.BlockSpec(memory_space=pltpu.VMEM)
    smem = pl.BlockSpec(memory_space=pltpu.SMEM)
    anywhere = pl.BlockSpec(memory_space=pl.ANY)
    return pl.pallas_call(
        functools.partial(step_kernel, sizes, gather_chunks, reduce_chunks, scale),
        out_shape=(pltpu.VMEM(tokens.shape, jnp.bfloat16),)
        + (pltpu.VMEM((owned,) + tile, jnp.float32),) * 3,
        in_specs=[anywhere] * 5 + [vmem] * 3 + [smem],
        out_specs=(vmem,) * 4,
        scratch_shapes=shapes,
        compiler_params=pltpu.CompilerParams(
            collective_id=0, has_side_effects=True, vmem_limit_bytes=49 * 1024 * 1024
        ),
    )(weights, first, second, tokens, grad_out, mask, regrown, last_step, step_now)


def copy_out(*refs):
    count = len(refs) // 2
    copies = [
        pltpu.make_async_copy(refs[at], refs[count + at], refs[-1].at[at])
        for at in range(count)
    ]
    for copy in copies:
        copy.start()
    for copy in copies:
        copy.wait()


def write_out(*arrays):
    return pl.pallas_call(
        copy_out,
        out_shape=tuple(jax.ShapeDtypeStruct(x.shape, x.dtype) for x in arrays),
        in_specs=[pl.BlockSpec(memory_space=pltpu.VMEM)] * len(arrays),
        out_specs=(pl.BlockSpec(memory_space=pl.ANY),) * len(arrays),
        scratch_shapes=[pltpu.SemaphoreType.DMA((len(arrays),))],
        compiler_params=pltpu.CompilerParams(vmem_limit_bytes=14 * 1024 * 1024),
    )(*arrays)


def per_device(
    tokens,
    grad_out,
    packed_weight_blocks,
    packed_first_moments,
    packed_second_moments,
    block_mask,
    last_step,
    regrown,
    step_now,
):
    scale_factor = 3.0 / math.sqrt(D)
    mask, fresh, last = (grid.transpose(0, 2, 1) for grid in (block_mask, regrown, last_step))
    results = run_step(
        packed_weight_blocks,
        packed_first_moments,
        packed_second_moments,
        tokens,
        grad_out,
        mask,
        fresh,
        last,
        step_now,
        scale_factor,
    )
    return write_out(*results)


def solution(mesh):
    in_specs = (
        P("dp", "tensor"),
        P("dp", "tensor"),
        P(("dp", "tensor"), None, None),
        P(("dp", "tensor"), None, None),
        P(("dp", "tensor"), None, None),
        P(None, None, "tensor"),
        P(None, None, "tensor"),
        P(None, None, "tensor"),
        P(),
    )
    out_specs = (
        P("dp", "tensor"),
        P(("dp", "tensor"), None, None),
        P(("dp", "tensor"), None, None),
        P(("dp", "tensor"), None, None),
    )
    return jax.shard_map(
        per_device, mesh=mesh, in_specs=in_specs, out_specs=out_specs, check_vma=False
    )
```
